128 devices in a mesh: req: 32 (over z, y, core), tp: 4 (over x).
Axes of the slice: x: 4, y: 4, z: 4, core: 2. Of those that a mesh axis runs over, the one named last changes fastest.
Arguments:
- tokens: bfloat16 [16384, 2048], P('req', 'tp')
- lengths: int32 [32, 16], P('req'), may hold values from 1 to 36, 512 in all within a row
- request_adapter_index: int32 [32, 16], P('req'), may hold values from 0 to 63, as said below
- attention_norm_gain: float32 [2048], replicated, may hold values from 0.5 to 1.5
- query_norm_gain: float32 [128], replicated, may hold values from 0.5 to 1.5
- key_norm_gain: float32 [128], replicated, may hold values from 0.5 to 1.5
- feedforward_norm_gain: float32 [2048], replicated, may hold values from 0.5 to 1.5
- query_weight: bfloat16 [2048, 2048], P(None, 'tp'), may hold values from -0.125 to 0.125
- key_weight: bfloat16 [2048, 1024], P(None, 'tp'), may hold values from -0.125 to 0.125
- value_weight: bfloat16 [2048, 1024], P(None, 'tp'), may hold values from -0.125 to 0.125
- output_weight: bfloat16 [2048, 2048], P('tp'), may hold values from -0.125 to 0.125
- gate_weight: bfloat16 [2048, 3072], P(None, 'tp'), may hold values from -0.125 to 0.125
- up_weight: bfloat16 [2048, 3072], P(None, 'tp'), may hold values from -0.125 to 0.125
- down_weight: bfloat16 [3072, 2048], P('tp'), may hold values from -0.109375 to 0.109375
- query_key_value_adapter_input: bfloat16 [64, 48, 2048], P('req', None, 'tp'), may hold values from -0.125 to 0.125
- output_adapter_input: bfloat16 [64, 16, 2048], P('req', None, 'tp'), may hold values from -0.125 to 0.125
- gate_up_adapter_input: bfloat16 [64, 32, 2048], P('req', None, 'tp'), may hold values from -0.125 to 0.125
- down_adapter_input: bfloat16 [64, 16, 3072], P('req', None, 'tp'), may hold values from -0.109375 to 0.109375
- query_adapter_output: bfloat16 [64, 16, 2048], P('req', None, 'tp'), may hold values from -1.5 to 1.5
- key_adapter_output: bfloat16 [64, 16, 1024], P('req', None, 'tp'), may hold values from -1.5 to 1.5
- value_adapter_output: bfloat16 [64, 16, 1024], P('req', None, 'tp'), may hold values from -1.5 to 1.5
- projection_adapter_output: bfloat16 [64, 16, 2048], P('req', None, 'tp'), may hold values from -1.5 to 1.5
- gate_adapter_output: bfloat16 [64, 16, 3072], P('req', None, 'tp'), may hold values from -1.5 to 1.5
- up_adapter_output: bfloat16 [64, 16, 3072], P('req', None, 'tp'), may hold values from -1.5 to 1.5
- down_adapter_output: bfloat16 [64, 16, 2048], P('req', None, 'tp'), may hold values from -1.5 to 1.5
Outputs:
- layer_out: bfloat16 [16384, 2048], P('req', 'tp')
The draws below stay inside these ranges and needn't reach their ends.
Inputs may be any that keep to these rules, and one draw needn't show every extreme that they name: `request_adapter_index`: the 16 requests of one group use adapters of 16 different owners; adapter a belongs to owner a // 2, the index of req that holds it. The lengths of one group's requests sum to 512; the longest is 36.
All inputs are finite; a program needn't handle non-finite values.
Results may differ from the reference program's by a relative error of at most 0.014.
Values may be sent and summed in bfloat16 or wider, within the bound.
A program may use at most 128 MiB of HBM per device.

```python
import math
import jax
import jax.numpy as jnp
import numpy as np
from jax import lax

MODEL_WIDTH = 2048
QUERY_HEADS = 16
KEY_VALUE_HEADS = 8
HEAD_WIDTH = 128
FEEDFWD_HALF = 3072
ADAPTER_RANK = 16
ADPT_DEV = 2
TOK_DEV = 512
REQ_DEV = 16
MOST_LEN = 36
GROUPS = 32
ADAPTER_TOTAL = 64
TOKENS = 16384


def draw_tokens(key, part):
    first_key, second_key, third_key = jax.random.split(jax.random.fold_in(key, 11), 3)
    column_scale = jnp.exp(jax.random.uniform(second_key, (MODEL_WIDTH,), jnp.float32, math.log(0.3), math.log(3.0)))
    row_scale = jnp.exp(jax.random.uniform(third_key, (TOKENS, 1), jnp.float32, math.log(0.5), math.log(2.0)))
    base_values = jax.random.normal(first_key, (TOKENS, MODEL_WIDTH), jnp.float32)
    return (base_values * column_scale[None, :] * row_scale).astype(jnp.bfloat16)


def draw_request_adapter_index(key, part):
    first_key, second_key = jax.random.split(jax.random.fold_in(key, 23), 2)
    owner_count = ADAPTER_TOTAL // ADPT_DEV
    scores = jax.random.randint(first_key, (GROUPS, owner_count), 0, 1 << 20) * owner_count
    scores = scores + jnp.arange(owner_count, dtype=jnp.int32)[None, :]
    order = jnp.argsort(scores, axis=1)[:, :REQ_DEV].astype(jnp.int32)
    local_pick = jax.random.randint(second_key, (GROUPS, REQ_DEV), 0, ADPT_DEV)
    return (order * ADPT_DEV + local_pick).astype(jnp.int32)


def block_levels(rng, dims, cuts, low, largest):
    factor_of = 1.0
    for dim, parts in cuts:
        heights = jax.random.uniform(jax.random.fold_in(jax.random.fold_in(rng, 6), dim), (parts,), jnp.float32, low / len(cuts), largest / len(cuts))
        factor_of = factor_of * jnp.repeat(jnp.exp(heights), dims[dim] // parts).reshape((-1,) + (1,) * (len(dims) - 1 - dim))
    return factor_of


def length_profile(count, total, most, skew):
    loads = [(1 << 20) // math.isqrt(rank ** skew) + 1 for rank in range(2, count + 1)]
    spare, given = total - most - (count - 1), [1] * (count - 1)
    while spare > 0:
        movable = [i for i in range(count - 1) if given[i] < most]
        pool, budget = sum([loads[i] for i in movable]), spare
        for i in movable:
            more = min(most - given[i], max(1, budget * loads[i] // pool), spare)
            given[i] = given[i] + more
            spare = spare - more
    return np.array([most] + given)


def uneven(rng, number_of, total, reach, lean):
    if number_of == 2:
        one = jax.random.randint(rng, (), max(1, total - reach), min(reach, total - 1) + 1)
        return jnp.stack([one, total - one])
    sizes = jnp.asarray(length_profile(number_of, total, reach, lean), jnp.int32)
    couples = (number_of - 1) // 2
    giver, receiver = sizes[1:1 + 2 * couples:2], sizes[2:2 + 2 * couples:2]
    room = jnp.minimum(giver - 1, reach - receiver)
    shifted = jax.random.randint(jax.random.fold_in(rng, 1), (couples,), 0, 1 << 20) % (room + 1)
    sizes = sizes.at[1:1 + 2 * couples:2].set(giver - shifted).at[2:2 + 2 * couples:2].set(receiver + shifted)
    return sizes[jax.random.permutation(jax.random.fold_in(rng, 2), number_of)]


def scatter_about(rng, shape, width, limit, shards=(), kind=jnp.bfloat16):
    entries = jax.random.normal(rng, shape, jnp.float32) * width
    if len(shards) > 0:
        entries = block_levels(rng, shape, shards, -0.22, 0.18) * entries
    return jnp.clip(entries, min=-limit, max=limit).astype(kind)


def setup_inputs(seed: int = 0) -> dict:
    streams_of = jax.random.split(jax.random.key(seed), 26)
    tokens = draw_tokens(jax.random.fold_in(streams_of[25], 71), 0)
    lengths = jax.vmap(lambda own: uneven(own, REQ_DEV, TOK_DEV, MOST_LEN, 2))(jax.random.split(streams_of[1], GROUPS)).reshape((GROUPS, REQ_DEV)).astype(jnp.int32)
    request_adapter_index = draw_request_adapter_index(jax.random.fold_in(streams_of[25], 71), 0)
    attention_norm_gain = jnp.clip(1.0 + 0.1 * jax.random.normal(streams_of[3], (MODEL_WIDTH,), jnp.float32), 0.5, 1.5)
    query_norm_gain = jnp.clip(1.0 + 0.1 * jax.random.normal(streams_of[4], (HEAD_WIDTH,), jnp.float32), 0.5, 1.5)
    key_norm_gain = jnp.clip(1.0 + 0.1 * jax.random.normal(streams_of[5], (HEAD_WIDTH,), jnp.float32), 0.5, 1.5)
    feedforward_norm_gain = jnp.clip(1.0 + 0.1 * jax.random.normal(streams_of[6], (MODEL_WIDTH,), jnp.float32), 0.5, 1.5)
    query_weight = scatter_about(streams_of[7], (MODEL_WIDTH, QUERY_HEADS * HEAD_WIDTH), MODEL_WIDTH ** -0.5, 0.125, ((1, 4),))
    key_weight = scatter_about(streams_of[8], (MODEL_WIDTH, KEY_VALUE_HEADS * HEAD_WIDTH), MODEL_WIDTH ** -0.5, 0.125, ((1, 4),))
    value_weight = scatter_about(streams_of[9], (MODEL_WIDTH, KEY_VALUE_HEADS * HEAD_WIDTH), MODEL_WIDTH ** -0.5, 0.125, ((1, 4),))
    output_weight = scatter_about(streams_of[10], (QUERY_HEADS * HEAD_WIDTH, MODEL_WIDTH), (QUERY_HEADS * HEAD_WIDTH) ** -0.5, 0.125, ((0, 4),))
    gate_weight = scatter_about(streams_of[11], (MODEL_WIDTH, FEEDFWD_HALF), MODEL_WIDTH ** -0.5, 0.125, ((1, 4),))
    up_weight = scatter_about(streams_of[12], (MODEL_WIDTH, FEEDFWD_HALF), MODEL_WIDTH ** -0.5, 0.125, ((1, 4),))
    down_weight = scatter_about(streams_of[13], (FEEDFWD_HALF, MODEL_WIDTH), FEEDFWD_HALF ** -0.5, 0.109375, ((0, 4),))
    query_key_value_adapter_input = scatter_about(streams_of[14], (ADAPTER_TOTAL, 3 * ADAPTER_RANK, MODEL_WIDTH), MODEL_WIDTH ** -0.5, 0.125, ((0, 32), (2, 4)))
    output_adapter_input = scatter_about(streams_of[15], (ADAPTER_TOTAL, ADAPTER_RANK, QUERY_HEADS * HEAD_WIDTH), (QUERY_HEADS * HEAD_WIDTH) ** -0.5, 0.125, ((0, 32), (2, 4)))
    gate_up_adapter_input = scatter_about(streams_of[16], (ADAPTER_TOTAL, 2 * ADAPTER_RANK, MODEL_WIDTH), MODEL_WIDTH ** -0.5, 0.125, ((0, 32), (2, 4)))
    down_adapter_input = scatter_about(streams_of[17], (ADAPTER_TOTAL, ADAPTER_RANK, FEEDFWD_HALF), FEEDFWD_HALF ** -0.5, 0.109375, ((0, 32), (2, 4)))
    query_adapter_output = scatter_about(streams_of[18], (ADAPTER_TOTAL, ADAPTER_RANK, QUERY_HEADS * HEAD_WIDTH), ADAPTER_RANK ** -0.5, 1.5, ((0, 32), (2, 4)))
    key_adapter_output = scatter_about(streams_of[19], (ADAPTER_TOTAL, ADAPTER_RANK, KEY_VALUE_HEADS * HEAD_WIDTH), ADAPTER_RANK ** -0.5, 1.5, ((0, 32), (2, 4)))
    value_adapter_output = scatter_about(streams_of[20], (ADAPTER_TOTAL, ADAPTER_RANK, KEY_VALUE_HEADS * HEAD_WIDTH), ADAPTER_RANK ** -0.5, 1.5, ((0, 32), (2, 4)))
    projection_adapter_output = scatter_about(streams_of[21], (ADAPTER_TOTAL, ADAPTER_RANK, MODEL_WIDTH), ADAPTER_RANK ** -0.5, 1.5, ((0, 32), (2, 4)))
    gate_adapter_output = scatter_about(streams_of[22], (ADAPTER_TOTAL, ADAPTER_RANK, FEEDFWD_HALF), ADAPTER_RANK ** -0.5, 1.5, ((0, 32), (2, 4)))
    up_adapter_output = scatter_about(streams_of[23], (ADAPTER_TOTAL, ADAPTER_RANK, FEEDFWD_HALF), ADAPTER_RANK ** -0.5, 1.5, ((0, 32), (2, 4)))
    down_adapter_output = scatter_about(streams_of[24], (ADAPTER_TOTAL, ADAPTER_RANK, MODEL_WIDTH), ADAPTER_RANK ** -0.5, 1.5, ((0, 32), (2, 4)))
    return dict(tokens=tokens, lengths=lengths, request_adapter_index=request_adapter_index, attention_norm_gain=attention_norm_gain, query_norm_gain=query_norm_gain, key_norm_gain=key_norm_gain, feedforward_norm_gain=feedforward_norm_gain, query_weight=query_weight, key_weight=key_weight, value_weight=value_weight, output_weight=output_weight, gate_weight=gate_weight, up_weight=up_weight, down_weight=down_weight, query_key_value_adapter_input=query_key_value_adapter_input, output_adapter_input=output_adapter_input, gate_up_adapter_input=gate_up_adapter_input, down_adapter_input=down_adapter_input, query_adapter_output=query_adapter_output, key_adapter_output=key_adapter_output, value_adapter_output=value_adapter_output, projection_adapter_output=projection_adapter_output, gate_adapter_output=gate_adapter_output, up_adapter_output=up_adapter_output, down_adapter_output=down_adapter_output)


epsilon = 1e-06
rope_base = 1000000.0

def rms_scale(values, gain):
    mean_square = lax.optimization_barrier(jnp.mean(values * values, axis=-1, keepdims=True))
    return values * lax.rsqrt(mean_square + epsilon) * gain

def rotate(values, position):
    head_size = values.shape[-1]
    half_size = head_size // 2
    inverse = rope_base ** (-(jnp.arange(half_size, dtype=jnp.float32) * 2.0) / head_size)
    angle = position[:, None] * inverse[None, :]
    cosine = jnp.cos(angle)[:, None, :]
    sine = jnp.sin(angle)[:, None, :]
    first_half = values[..., :half_size]
    second_half = values[..., half_size:]
    return jnp.concatenate([first_half * cosine - second_half * sine, second_half * cosine + first_half * sine], axis=-1)

def request_layout(request_lens, row_count):
    ends = jnp.cumsum(request_lens).astype(jnp.int32)
    starts = (ends - request_lens).astype(jnp.int32)
    row_index = jnp.arange(row_count, dtype=jnp.int32)
    membership_mask = (row_index[:, None] >= starts[None, :]) & (row_index[:, None] < ends[None, :])
    member_int = membership_mask.astype(jnp.int32)
    request = lax.optimization_barrier(jnp.sum(member_int * jnp.arange(request_lens.shape[0], dtype=jnp.int32)[None, :], axis=1))
    position = row_index - lax.optimization_barrier(jnp.sum(member_int * starts[None, :], axis=1))
    return (membership_mask, request, position)

def adapter_update(inputs, membership_mask, a_rows, b_list):
    low_rank = jnp.einsum('tw,jrw->tjr', inputs.astype(jnp.float32), a_rows.astype(jnp.float32))
    low_rank = (low_rank * membership_mask.astype(jnp.float32)[:, :, None]).astype(jnp.bfloat16)
    deltas = []
    offset = 0
    for b_rows in b_list:
        rank_width = b_rows.shape[1]
        piece = low_rank[:, :, offset:offset + rank_width].astype(jnp.float32)
        deltas.append(jnp.einsum('tjr,jro->to', piece, b_rows.astype(jnp.float32)).astype(jnp.bfloat16))
        offset += rank_width
    return deltas

def attend(query, keys, values, request):
    row_count, query_heads, head_size = query.shape
    kv_heads = keys.shape[1]
    grouped = query.reshape(row_count, kv_heads, query_heads // kv_heads, head_size)
    scores = jnp.einsum('tkgd,skd->kgts', grouped.astype(jnp.float32), keys.astype(jnp.float32)) / math.sqrt(head_size)
    row_index = jnp.arange(row_count, dtype=jnp.int32)
    allowed = (request[:, None] == request[None, :]) & (row_index[None, :] <= row_index[:, None])
    raw = jnp.where(allowed[None, None], jnp.exp(scores), 0.0)
    probs = (raw / lax.optimization_barrier(jnp.sum(raw, axis=-1, keepdims=True))).astype(jnp.bfloat16)
    mixed = jnp.einsum('kgts,skd->tkgd', probs.astype(jnp.float32), values.astype(jnp.float32))
    return mixed.reshape(row_count, query_heads * head_size).astype(jnp.bfloat16)

def reference(tokens, lengths, request_adapter_index, attention_norm_gain, query_norm_gain, key_norm_gain, feedforward_norm_gain, query_weight, key_weight, value_weight, output_weight, gate_weight, up_weight, down_weight, query_key_value_adapter_input, output_adapter_input, gate_up_adapter_input, down_adapter_input, query_adapter_output, key_adapter_output, value_adapter_output, projection_adapter_output, gate_adapter_output, up_adapter_output, down_adapter_output):
    blocks = tokens.reshape(GROUPS, TOK_DEV, MODEL_WIDTH)

    def one_block(items):
        block, request_lens, request_index_list = items
        membership_mask, request, position = request_layout(request_lens, TOK_DEV)
        pos_float = position.astype(jnp.float32)
        attention_normalized = rms_scale(block.astype(jnp.float32), attention_norm_gain).astype(jnp.bfloat16)
        query_update, key_update, value_update = adapter_update(attention_normalized, membership_mask, query_key_value_adapter_input[request_index_list], [query_adapter_output[request_index_list], key_adapter_output[request_index_list], value_adapter_output[request_index_list]])
        query = jnp.dot(attention_normalized, query_weight, preferred_element_type=jnp.float32) + query_update.astype(jnp.float32)
        query = rotate(rms_scale(query.reshape(TOK_DEV, QUERY_HEADS, HEAD_WIDTH), query_norm_gain), pos_float).astype(jnp.bfloat16)
        keys = jnp.dot(attention_normalized, key_weight, preferred_element_type=jnp.float32) + key_update.astype(jnp.float32)
        keys = rotate(rms_scale(keys.reshape(TOK_DEV, KEY_VALUE_HEADS, HEAD_WIDTH), key_norm_gain), pos_float).astype(jnp.bfloat16)
        values = (jnp.dot(attention_normalized, value_weight, preferred_element_type=jnp.float32) + value_update.astype(jnp.float32)).astype(jnp.bfloat16)
        attention_result = attend(query, keys, values.reshape(TOK_DEV, KEY_VALUE_HEADS, HEAD_WIDTH), request)
        output_update = adapter_update(attention_result, membership_mask, output_adapter_input[request_index_list], [projection_adapter_output[request_index_list]])[0]
        resid = jnp.dot(attention_result, output_weight, preferred_element_type=jnp.float32) + output_update.astype(jnp.float32) + block.astype(jnp.float32)
        resid = resid.astype(jnp.bfloat16)
        feedforward_normalized = rms_scale(resid.astype(jnp.float32), feedforward_norm_gain).astype(jnp.bfloat16)
        gate_update, up_update = adapter_update(feedforward_normalized, membership_mask, gate_up_adapter_input[request_index_list], [gate_adapter_output[request_index_list], up_adapter_output[request_index_list]])
        gate = jnp.dot(feedforward_normalized, gate_weight, preferred_element_type=jnp.float32) + gate_update.astype(jnp.float32)
        upward = jnp.dot(feedforward_normalized, up_weight, preferred_element_type=jnp.float32) + up_update.astype(jnp.float32)
        hidden_state = (jax.nn.silu(gate) * upward).astype(jnp.bfloat16)
        down_update = adapter_update(hidden_state, membership_mask, down_adapter_input[request_index_list], [down_adapter_output[request_index_list]])[0]
        result = jnp.dot(hidden_state, down_weight, preferred_element_type=jnp.float32) + down_update.astype(jnp.float32) + resid.astype(jnp.float32)
        return result.astype(jnp.bfloat16)
    outputs = lax.map(one_block, (blocks, lengths, request_adapter_index))
    return outputs.reshape(TOKENS, MODEL_WIDTH)
```

```python
import math

import jax
import jax.numpy as jnp
from jax import lax
from jax.experimental import pallas as pl
from jax.experimental.pallas import tpu as pltpu
from jax.sharding import PartitionSpec as P

HEAD_WIDTH = 128


epsilon = 1e-06
rope_base = 1000000.0


def rms_scale(values, gain):
    mean_square = jnp.mean(values * values, axis=-1, keepdims=True)
    return values * lax.rsqrt(mean_square + epsilon) * gain


def rotate(values, position):
    head_size = values.shape[-1]
    half_size = head_size // 2
    inverse = rope_base ** (-(jnp.arange(half_size, dtype=jnp.float32) * 2.0) / head_size)
    angle = position[:, None] * inverse[None, :]
    cosine = jnp.cos(angle)[:, None, :]
    sine = jnp.sin(angle)[:, None, :]
    first_half = values[..., :half_size]
    second_half = values[..., half_size:]
    return jnp.concatenate(
        [first_half * cosine - second_half * sine, second_half * cosine + first_half * sine],
        axis=-1,
    )


def request_layout(request_lens, row_count):
    ends = jnp.cumsum(request_lens)
    starts = ends - request_lens
    row_index = jnp.arange(row_count, dtype=jnp.int32)
    membership_mask = (row_index[:, None] >= starts[None, :]) & (row_index[:, None] < ends[None, :])
    member_int = membership_mask.astype(jnp.int32)
    request = jnp.sum(
        member_int * jnp.arange(request_lens.shape[0], dtype=jnp.int32)[None, :], axis=1
    )
    position = row_index - jnp.sum(member_int * starts[None, :], axis=1)
    return (member_int, request, position, starts)


def attend(query, keys, values, request):
    row_count, query_heads, head_size = query.shape
    kv_heads = keys.shape[1]
    grouped = query.reshape(row_count, kv_heads, query_heads // kv_heads, head_size)
    scores = jnp.einsum(
        "tkgd,skd->kgts", grouped, keys, preferred_element_type=jnp.float32
    ) / math.sqrt(head_size)
    row_index = jnp.arange(row_count, dtype=jnp.int32)
    allowed = (request[:, None] == request[None, :]) & (row_index[None, :] <= row_index[:, None])
    raw = jnp.where(allowed[None, None], jnp.exp(scores), 0.0)
    probs = (raw / jnp.sum(raw, axis=-1, keepdims=True)).astype(jnp.bfloat16)
    mixed = jnp.einsum("kgts,skd->tkgd", probs, values, preferred_element_type=jnp.float32)
    return mixed.reshape(row_count, query_heads * head_size).astype(jnp.bfloat16)


def gather_features(shard):
    return lax.all_gather(shard, "tp", axis=1, tiled=True)


def reduce_columns(term):
    return lax.psum_scatter(term, "tp", scatter_dimension=1, tiled=True)


def pick_kernel(pick_ref, table_ref, *out_refs):
    offset = 0
    for out_ref in out_refs:
        rows = out_ref.shape[1]
        out_ref[...] = table_ref[:, offset : offset + rows, :]
        offset += rows


def pick_adapters(table, index_list, row_counts):
    count = index_list.shape[0]
    rows, width = table.shape[1:]
    grid_spec = pltpu.PrefetchScalarGridSpec(
        num_scalar_prefetch=1,
        grid=(count,),
        in_specs=[pl.BlockSpec((1, rows, width), lambda i, pick: (pick[i], 0, 0))],
        out_specs=[pl.BlockSpec((1, n, width), lambda i, pick: (i, 0, 0)) for n in row_counts],
    )
    picked = pl.pallas_call(
        pick_kernel,
        grid_spec=grid_spec,
        out_shape=[jax.ShapeDtypeStruct((count, n, width), table.dtype) for n in row_counts],
        compiler_params=pltpu.CompilerParams(vmem_limit_bytes=8 << 20),
    )(index_list, table)
    return [part.reshape(-1, width) for part in picked]


def gather_owned(parts):
    return lax.all_gather(jnp.concatenate(parts, axis=1), "req", axis=0, tiled=True)


def low_product(inputs, a_rows, own):
    low = lax.dot_general(
        inputs, a_rows, (((1,), (1,)), ((), ())), preferred_element_type=jnp.float32
    )
    return jnp.where(own, low, 0.0).astype(jnp.bfloat16)


def product(left, right):
    return jnp.dot(left, right, preferred_element_type=jnp.float32)


def per_device(
    tokens,
    lengths,
    request_adapter_index,
    attention_norm_gain,
    query_norm_gain,
    key_norm_gain,
    feedforward_norm_gain,
    query_weight,
    key_weight,
    value_weight,
    output_weight,
    gate_weight,
    up_weight,
    down_weight,
    query_key_value_adapter_input,
    output_adapter_input,
    gate_up_adapter_input,
    down_adapter_input,
    query_adapter_output,
    key_adapter_output,
    value_adapter_output,
    projection_adapter_output,
    gate_adapter_output,
    up_adapter_output,
    down_adapter_output,
):
    row_count = tokens.shape[0]
    request_lens = lengths[0]
    request_index_list = request_adapter_index[0]
    member_int, request, position, starts = request_layout(request_lens, row_count)
    pos_float = position.astype(jnp.float32)
    rank = query_adapter_output.shape[1]
    request_count = request_lens.shape[0]
    column_request = jnp.arange(request_count * rank, dtype=jnp.int32) // rank
    own = request[:, None] == column_request[None, :]

    whole = gather_features(tokens)
    table_one = gather_owned(
        [
            query_key_value_adapter_input,
            query_adapter_output,
            jnp.concatenate([key_adapter_output, value_adapter_output], axis=2),
        ]
    )
    table_two = gather_owned(
        [
            output_adapter_input,
            projection_adapter_output,
            gate_up_adapter_input,
            down_adapter_output,
        ]
    )
    table_three = gather_owned([gate_adapter_output, up_adapter_output, down_adapter_input])
    a_qkv, b_query, b_kv = pick_adapters(table_one, request_index_list, (3 * rank, rank, rank))
    a_qkv = gather_features(a_qkv)
    a_out, b_out, a_gate_up, b_down = pick_adapters(
        table_two, request_index_list, (rank, rank, 2 * rank, rank)
    )
    b_gate, b_up, a_down = pick_adapters(table_three, request_index_list, (rank, rank, rank))
    spread = gather_features(
        jnp.concatenate([a_gate_up, b_out, b_down], axis=0)
    )
    pair_rows = 2 * rank * request_count
    single_rows = rank * request_count
    a_gate_up = spread[:pair_rows].reshape(request_count, 2, rank, -1)
    b_out = spread[pair_rows : pair_rows + single_rows]
    b_down = spread[pair_rows + single_rows :]
    a_qkv = a_qkv.reshape(request_count, 3, rank, -1)

    def part(stack, number):
        return stack[:, number].reshape(single_rows, -1)

    normed = rms_scale(whole.astype(jnp.float32), attention_norm_gain).astype(jnp.bfloat16)
    kv_width = key_weight.shape[1]
    query = product(normed, query_weight) + product(
        low_product(normed, part(a_qkv, 0), own), b_query
    )
    heads_here = query.shape[1] // HEAD_WIDTH
    query = rotate(
        rms_scale(query.reshape(row_count, heads_here, HEAD_WIDTH), query_norm_gain), pos_float
    ).astype(jnp.bfloat16)
    keys = product(normed, key_weight) + product(
        low_product(normed, part(a_qkv, 1), own), b_kv[:, :kv_width]
    )
    kv_here = keys.shape[1] // HEAD_WIDTH
    keys = rotate(
        rms_scale(keys.reshape(row_count, kv_here, HEAD_WIDTH), key_norm_gain), pos_float
    ).astype(jnp.bfloat16)
    values = (
        product(normed, value_weight)
        + product(low_product(normed, part(a_qkv, 2), own), b_kv[:, kv_width:])
    ).astype(jnp.bfloat16)
    attended = attend(query, keys, values.reshape(row_count, kv_here, HEAD_WIDTH), request)
    share = product(attended, output_weight) + product(low_product(attended, a_out, own), b_out)
    summed = reduce_columns(share.astype(jnp.bfloat16))
    resid = (summed.astype(jnp.float32) + tokens.astype(jnp.float32)).astype(jnp.bfloat16)
    whole_two = gather_features(resid)
    normed_two = rms_scale(whole_two.astype(jnp.float32), feedforward_norm_gain).astype(
        jnp.bfloat16
    )
    gate = product(normed_two, gate_weight) + product(
        low_product(normed_two, part(a_gate_up, 0), own), b_gate
    )
    upward = product(normed_two, up_weight) + product(
        low_product(normed_two, part(a_gate_up, 1), own), b_up
    )
    hidden = (jax.nn.silu(gate) * upward).astype(jnp.bfloat16)
    share_two = product(hidden, down_weight) + product(low_product(hidden, a_down, own), b_down)
    summed_two = reduce_columns(share_two.astype(jnp.bfloat16))
    return (summed_two.astype(jnp.float32) + resid.astype(jnp.float32)).astype(jnp.bfloat16)


def solution(mesh):
    placed = (
        P("req", "tp"),
        P("req", None),
        P("req", None),
        P(),
        P(),
        P(),
        P(),
        P(None, "tp"),
        P(None, "tp"),
        P(None, "tp"),
        P("tp", None),
        P(None, "tp"),
        P(None, "tp"),
        P("tp", None),
        P("req", None, "tp"),
        P("req", None, "tp"),
        P("req", None, "tp"),
        P("req", None, "tp"),
        P("req", None, "tp"),
        P("req", None, "tp"),
        P("req", None, "tp"),
        P("req", None, "tp"),
        P("req", None, "tp"),
        P("req", None, "tp"),
        P("req", None, "tp"),
    )
    return jax.shard_map(
        per_device, mesh=mesh, in_specs=placed, out_specs=P("req", "tp"), check_vma=False
    )
```

```python
import math

import jax
import jax.numpy as jnp
from jax import lax
from jax.experimental import pallas as pl
from jax.experimental.pallas import tpu as pltpu
from jax.sharding import PartitionSpec as P

HEAD_WIDTH = 128
LANES = 128


epsilon = 1e-06
rope_base = 1000000.0


def rms_scale(values, gain):
    mean_square = jnp.mean(values * values, axis=-1, keepdims=True)
    return values * lax.rsqrt(mean_square + epsilon) * gain


def rotate(values, position):
    head_size = values.shape[-1]
    half_size = head_size // 2
    inverse = rope_base ** (-(jnp.arange(half_size, dtype=jnp.float32) * 2.0) / head_size)
    angle = position[:, None] * inverse[None, :]
    cosine = jnp.cos(angle)[:, None, :]
    sine = jnp.sin(angle)[:, None, :]
    first_half = values[..., :half_size]
    second_half = values[..., half_size:]
    return jnp.concatenate(
        [first_half * cosine - second_half * sine, second_half * cosine + first_half * sine],
        axis=-1,
    )


def request_layout(request_lens, row_count):
    ends = jnp.cumsum(request_lens)
    starts = ends - request_lens
    row_index = jnp.arange(row_count, dtype=jnp.int32)
    membership_mask = (row_index[:, None] >= starts[None, :]) & (row_index[:, None] < ends[None, :])
    member_int = membership_mask.astype(jnp.int32)
    request = jnp.sum(
        member_int * jnp.arange(request_lens.shape[0], dtype=jnp.int32)[None, :], axis=1
    )
    position = row_index - jnp.sum(member_int * starts[None, :], axis=1)
    return (member_int, request, position, starts)


def attend(query, keys, values, request):
    row_count, query_heads, head_size = query.shape
    kv_heads = keys.shape[1]
    grouped = query.reshape(row_count, kv_heads, query_heads // kv_heads, head_size)
    scores = jnp.einsum(
        "tkgd,skd->kgts", grouped, keys, preferred_element_type=jnp.float32
    ) / math.sqrt(head_size)
    row_index = jnp.arange(row_count, dtype=jnp.int32)
    allowed = (request[:, None] == request[None, :]) & (row_index[None, :] <= row_index[:, None])
    raw = jnp.where(allowed[None, None], jnp.exp(scores), 0.0)
    probs = (raw / jnp.sum(raw, axis=-1, keepdims=True)).astype(jnp.bfloat16)
    mixed = jnp.einsum("kgts,skd->tkgd", probs, values, preferred_element_type=jnp.float32)
    return mixed.reshape(row_count, query_heads * head_size).astype(jnp.bfloat16)


def ring_kernel(block_ref, whole_ref, local_sem, send_sems, recv_sems):
    ring = lax.axis_size("tp")
    req, me = lax.axis_index("req"), lax.axis_index("tp")
    right, left = lax.rem(me + 1, ring), lax.rem(me + ring - 1, ring)
    rows, width = block_ref.shape
    half = rows // 2

    def columns(owner, first, count):
        return whole_ref.at[pl.ds(first, count), pl.ds(pl.multiple_of(owner * width, width), width)]

    def send(source, target, number, peer):
        return pltpu.make_async_remote_copy(
            src_ref=source,
            dst_ref=target,
            send_sem=send_sems.at[number],
            recv_sem=recv_sems.at[number],
            device_id=(req, peer),
            device_id_type=pl.DeviceIdType.MESH,
        )

    barrier = pltpu.get_barrier_semaphore()
    for peer in (left, right):
        pl.semaphore_signal(
            barrier, inc=1, device_id=(req, peer), device_id_type=pl.DeviceIdType.MESH
        )
    pl.semaphore_wait(barrier, 2)
    mine = columns(me, 0, rows)
    to_right = send(block_ref, mine, 0, right)
    to_left = send(block_ref, mine, 1, left)
    to_right.start()
    to_left.start()
    local = pltpu.make_async_copy(block_ref, mine, local_sem)
    local.start()
    to_right.wait_recv()
    top = columns(left, 0, half)
    on_right = send(top, top, 2, right)
    on_right.start()
    to_left.wait_recv()
    bottom = columns(right, half, half)
    on_left = send(bottom, bottom, 3, left)
    on_left.start()
    local.wait()
    to_right.wait_send()
    to_left.wait_send()
    on_right.wait()
    on_left.wait()


def ring_gather(block, call_number):
    rows, width = block.shape
    return pl.pallas_call(
        ring_kernel,
        out_shape=jax.ShapeDtypeStruct((rows, width * lax.axis_size("tp")), block.dtype),
        in_specs=[pl.BlockSpec(memory_space=pltpu.VMEM)],
        out_specs=pl.BlockSpec(memory_space=pl.ANY),
        scratch_shapes=[
            pltpu.SemaphoreType.DMA,
            pltpu.SemaphoreType.DMA((4,)),
            pltpu.SemaphoreType.DMA((4,)),
        ],
        compiler_params=pltpu.CompilerParams(
            collective_id=call_number, has_side_effects=True, vmem_limit_bytes=8 << 20
        ),
    )(block)


def reduce_columns(term):
    return lax.psum_scatter(term, "tp", scatter_dimension=1, tiled=True)


def pick_kernel(pick_ref, table_ref, *out_refs):
    offset = 0
    for out_ref in out_refs:
        rows = out_ref.shape[1]
        out_ref[...] = table_ref[:, offset : offset + rows, :]
        offset += rows


def pick_adapters(table, index_list, row_counts):
    count = index_list.shape[0]
    rows, width = table.shape[1:]
    grid_spec = pltpu.PrefetchScalarGridSpec(
        num_scalar_prefetch=1,
        grid=(count,),
        in_specs=[pl.BlockSpec((1, rows, width), lambda i, pick: (pick[i], 0, 0))],
        out_specs=[pl.BlockSpec((1, n, width), lambda i, pick: (i, 0, 0)) for n in row_counts],
    )
    picked = pl.pallas_call(
        pick_kernel,
        grid_spec=grid_spec,
        out_shape=[jax.ShapeDtypeStruct((count, n, width), table.dtype) for n in row_counts],
        compiler_params=pltpu.CompilerParams(vmem_limit_bytes=8 << 20),
    )(index_list, table)
    return picked


def gather_owned(parts):
    return lax.all_gather(jnp.concatenate(parts, axis=1), "req", axis=0, tiled=True)


def low_product(inputs, a_rows, own):
    low = lax.dot_general(
        inputs, a_rows, (((1,), (1,)), ((), ())), preferred_element_type=jnp.float32
    )
    return jnp.where(own, low, 0.0).astype(jnp.bfloat16)


def product(left, right):
    return jnp.dot(left, right, preferred_element_type=jnp.float32)


def shared_low(inputs, a_rows, request, rank, call_number):
    kinds = a_rows.shape[1] // rank
    rows = a_rows.shape[0] * a_rows.shape[1]
    slot = jnp.arange(rows, dtype=jnp.int32)
    own = request[:, None] == (slot // (kinds * rank))[None, :]
    low = low_product(inputs, a_rows.reshape(rows, -1), own)
    lane = jnp.arange(LANES, dtype=jnp.int32)
    fold = (slot % (kinds * rank))[:, None] == lane[None, :]
    partial = product(low, fold.astype(jnp.bfloat16)).astype(jnp.bfloat16)
    parts = ring_gather(partial, call_number)
    spread_slot = jnp.arange(a_rows.shape[0] * rank, dtype=jnp.int32)
    own_spread = request[:, None] == (spread_slot // rank)[None, :]
    source = jnp.arange(parts.shape[1], dtype=jnp.int32) % LANES
    lows = []
    for kind in range(kinds):
        expand = source[:, None] == (spread_slot % rank + kind * rank)[None, :]
        spread = product(parts, expand.astype(jnp.bfloat16))
        lows.append(jnp.where(own_spread, spread, 0.0).astype(jnp.bfloat16))
    return lows


def per_device(
    tokens,
    lengths,
    request_adapter_index,
    attention_norm_gain,
    query_norm_gain,
    key_norm_gain,
    feedforward_norm_gain,
    query_weight,
    key_weight,
    value_weight,
    output_weight,
    gate_weight,
    up_weight,
    down_weight,
    query_key_value_adapter_input,
    output_adapter_input,
    gate_up_adapter_input,
    down_adapter_input,
    query_adapter_output,
    key_adapter_output,
    value_adapter_output,
    projection_adapter_output,
    gate_adapter_output,
    up_adapter_output,
    down_adapter_output,
):
    row_count = tokens.shape[0]
    request_lens = lengths[0]
    request_index_list = request_adapter_index[0]
    member_int, request, position, starts = request_layout(request_lens, row_count)
    pos_float = position.astype(jnp.float32)
    rank = query_adapter_output.shape[1]
    feature_width = tokens.shape[1]
    first_feature = lax.axis_index("tp") * feature_width

    def own_features(values):
        return lax.dynamic_slice_in_dim(values, first_feature, feature_width, 1)

    def flat(table):
        return table.reshape(-1, table.shape[2])

    table_one = gather_owned(
        [
            query_key_value_adapter_input,
            query_adapter_output,
            jnp.concatenate([key_adapter_output, value_adapter_output], axis=2),
        ]
    )
    whole = ring_gather(tokens, 0)
    table_two = gather_owned(
        [
            output_adapter_input,
            projection_adapter_output,
            gate_up_adapter_input,
            down_adapter_output,
        ]
    )
    table_three = gather_owned([gate_adapter_output, up_adapter_output, down_adapter_input])
    a_qkv, b_query, b_kv = pick_adapters(table_one, request_index_list, (3 * rank, rank, rank))

    normed = rms_scale(whole.astype(jnp.float32), attention_norm_gain).astype(jnp.bfloat16)
    low_query, low_key, low_value = shared_low(own_features(normed), a_qkv, request, rank, 1)
    b_query, b_kv = flat(b_query), flat(b_kv)
    kv_width = key_weight.shape[1]
    query = product(normed, query_weight) + product(low_query, b_query)
    heads_here = query.shape[1] // HEAD_WIDTH
    query = rotate(
        rms_scale(query.reshape(row_count, heads_here, HEAD_WIDTH), query_norm_gain), pos_float
    ).astype(jnp.bfloat16)
    keys = product(normed, key_weight) + product(low_key, b_kv[:, :kv_width])
    kv_here = keys.shape[1] // HEAD_WIDTH
    keys = rotate(
        rms_scale(keys.reshape(row_count, kv_here, HEAD_WIDTH), key_norm_gain), pos_float
    ).astype(jnp.bfloat16)
    values = (product(normed, value_weight) + product(low_value, b_kv[:, kv_width:])).astype(
        jnp.bfloat16
    )
    attended = attend(query, keys, values.reshape(row_count, kv_here, HEAD_WIDTH), request)
    share = product(attended, output_weight).astype(jnp.bfloat16)
    share, table_two, table_three = lax.optimization_barrier((share, table_two, table_three))
    summed = reduce_columns(share)
    a_out, b_out, a_gate_up, b_down = pick_adapters(
        table_two, request_index_list, (rank, rank, 2 * rank, rank)
    )
    b_gate, b_up, a_down = pick_adapters(table_three, request_index_list, (rank, rank, rank))
    (low_out,) = shared_low(attended, a_out, request, rank, 2)
    resid = (
        summed.astype(jnp.float32) + product(low_out, flat(b_out)) + tokens.astype(jnp.float32)
    ).astype(jnp.bfloat16)
    whole_two = ring_gather(resid, 3)
    normed_two = rms_scale(whole_two.astype(jnp.float32), feedforward_norm_gain).astype(
        jnp.bfloat16
    )
    low_gate, low_up = shared_low(own_features(normed_two), a_gate_up, request, rank, 4)
    gate = product(normed_two, gate_weight) + product(low_gate, flat(b_gate))
    upward = product(normed_two, up_weight) + product(low_up, flat(b_up))
    hidden = (jax.nn.silu(gate) * upward).astype(jnp.bfloat16)
    summed_two = reduce_columns(product(hidden, down_weight).astype(jnp.bfloat16))
    (low_down,) = shared_low(hidden, a_down, request, rank, 5)
    return (
        summed_two.astype(jnp.float32)
        + product(low_down, flat(b_down))
        + resid.astype(jnp.float32)
    ).astype(jnp.bfloat16)


def solution(mesh):
    placed = (
        P("req", "tp"),
        P("req", None),
        P("req", None),
        P(),
        P(),
        P(),
        P(),
        P(None, "tp"),
        P(None, "tp"),
        P(None, "tp"),
        P("tp", None),
        P(None, "tp"),
        P(None, "tp"),
        P("tp", None),
        P("req", None, "tp"),
        P("req", None, "tp"),
        P("req", None, "tp"),
        P("req", None, "tp"),
        P("req", None, "tp"),
        P("req", None, "tp"),
        P("req", None, "tp"),
        P("req", None, "tp"),
        P("req", None, "tp"),
        P("req", None, "tp"),
        P("req", None, "tp"),
    )
    return jax.shard_map(
        per_device, mesh=mesh, in_specs=placed, out_specs=P("req", "tp"), check_vma=False
    )
```
